128 devices in a mesh: loop: 16 (over z_hi, y, core), tp: 8 (over z_lo, x).
Axes of the slice: x: 4, y: 4, z: 4 (z_hi: 2, z_lo: 2; z = z_hi * 2 + z_lo), core: 2. Of those that a mesh axis runs over, the one named last changes fastest.
Arguments:
- tokens: bfloat16 [4096, 4096], P('loop', 'tp'), may hold values from -6 to 6
- out_grad: bfloat16 [4096, 6144], P('loop', 'tp'), may hold values from -6 to 6
- qkv_weight: bfloat16 [3, 4096, 6144], P(None, 'loop', 'tp'), may hold values from -0.09375 to 0.09375
- dest_row: int32 [4096], P('loop'), may hold values from 0 to 383, as said below
- loop_modality: int32 [16], replicated, may hold values from 0 to 2, as said below
Outputs:
- projected: bfloat16 [4096, 6144], P('loop', 'tp')
- input_grad: bfloat16 [4096, 4096], P('loop', 'tp')
- weight_grad: bfloat16 [3, 4096, 6144], P(None, 'loop', 'tp')
The draws below stay inside these ranges and needn't reach their ends.
Inputs may be any that keep to these rules, and one draw needn't show every extreme that they name: `dest_row`: within each aligned block of 256 tokens the values are distinct, so at most 24 tokens of one block name one loop; in every draw some loop is named by exactly 24 tokens of every block. `loop_modality`: A quarter of the loops hold 0, half hold 1, a quarter hold 2.
All inputs are finite; a program needn't handle non-finite values.
Results may differ from the reference program's by a relative error of at most 0.014.
Values may be sent and summed in bfloat16 or wider, within the bound.
A program may use at most 128 MiB of HBM per device.

```python
import jax
import jax.numpy as jnp
from jax import lax

D = 4096
MODALITIES = 3
TOK_LOOP = 256
QKV = 6144
CAP = 24
TOKENS = 4096
N_LOOP = 16
N_TP = 8


def draw_loop_modality(key, part):
    shuffle = jax.random.permutation(key, N_LOOP)
    return jnp.where(shuffle < N_LOOP // 4, 0, jnp.where(shuffle < 3 * N_LOOP // 4, 1, 2)).astype(jnp.int32)


def draw_dest_row(key, part):
    slot_count = N_LOOP * CAP
    full_key = jax.random.fold_in(key, 7)
    bias_key = jax.random.fold_in(key, 11)
    target = jax.random.randint(full_key, (), 0, N_LOOP)
    loop_bias = jax.random.randint(bias_key, (N_LOOP,), 0, 32768)
    slot_ids = jnp.arange(slot_count, dtype=jnp.int32)
    slot_owner = slot_ids // CAP

    def one_source(source_index):
        source_key = jax.random.fold_in(key, 1000 + source_index)
        jitter = jax.random.randint(jax.random.fold_in(source_key, 1), (slot_count,), 0, 32768)
        priority = jitter + loop_bias[slot_owner] + jnp.where(slot_owner == target, 131072, 0) + jnp.where(slot_ids == slot_count - 1, 65536, 0)
        priority = priority * 8192 + slot_ids
        _, chosen = lax.top_k(priority, TOK_LOOP)
        shuffle = jax.random.permutation(jax.random.fold_in(source_key, 2), TOK_LOOP)
        return chosen[shuffle].astype(jnp.int32)
    return jax.vmap(one_source)(jnp.arange(N_LOOP, dtype=jnp.int32)).reshape(-1).astype(jnp.int32)


def block_scale(own_key, shape, cuts, smallest, largest):
    level = 1.0
    for axis_at, parts in cuts:
        heights = jax.random.uniform(jax.random.fold_in(jax.random.fold_in(own_key, 6), axis_at), (parts,), jnp.float32, smallest / len(cuts), largest / len(cuts))
        level = level * jnp.repeat(jnp.exp(heights), shape[axis_at] // parts).reshape((-1,) + (1,) * (len(shape) - 1 - axis_at))
    return level


def normal_values(key, dims, spread, reach, cuts=(), kind=jnp.bfloat16):
    drawn = spread * jax.random.normal(key, dims, jnp.float32)
    if cuts:
        drawn = drawn * block_scale(key, dims, cuts, -0.22, 0.18)
    return jnp.clip(drawn, -reach, reach).astype(kind)


def setup_inputs(seed: int = 0) -> dict:
    keys = jax.random.split(jax.random.key(seed), 6)
    tokens = normal_values(keys[0], (TOKENS, D), 1.0, 6.0, ((0, 16), (1, 8)))
    out_grad = normal_values(keys[1], (TOKENS, QKV), 1.0, 6.0, ((0, 16), (1, 8)))
    qkv_weight = normal_values(keys[2], (MODALITIES, D, QKV), D ** -0.5, 0.09375, ((1, 16), (2, 8)))
    dest_row = draw_dest_row(jax.random.fold_in(keys[5], 71), 0)
    loop_modality = draw_loop_modality(jax.random.fold_in(keys[5], 71), 0)
    return dict(tokens=tokens, out_grad=out_grad, qkv_weight=qkv_weight, dest_row=dest_row, loop_modality=loop_modality)


def reference(tokens, out_grad, qkv_weight, dest_row, loop_modality):
    slot_count = N_LOOP * CAP
    source = (jnp.arange(TOKENS, dtype=jnp.int32) // TOK_LOOP).astype(jnp.int32)
    target = (dest_row // CAP).astype(jnp.int32)
    position_index = (target * slot_count + source * CAP + dest_row % CAP).astype(jnp.int32)
    token_buffer = jnp.zeros((N_LOOP * slot_count, D), jnp.bfloat16).at[position_index].set(tokens)
    token_buffer = token_buffer.reshape(N_LOOP, slot_count, D)
    grad_buffer = jnp.zeros((N_LOOP * slot_count, QKV), jnp.bfloat16).at[position_index].set(out_grad)
    grad_buffer = grad_buffer.reshape(N_LOOP, slot_count, QKV)
    group_width = QKV // N_TP
    grad_scale = float(TOKENS) ** -0.5

    def loop_step(accumulated, loop_item):
        token_rows, grad_rows, modality = loop_item
        weight = lax.dynamic_index_in_dim(qkv_weight, modality, 0, keepdims=False)
        projected = jnp.dot(token_rows, weight, preferred_element_type=jnp.float32).astype(jnp.bfloat16)
        summed = jnp.zeros((slot_count, D), jnp.float32)
        for group_index in range(N_TP):
            lower = group_index * group_width
            group_term = lax.dot_general(grad_rows[:, lower:lower + group_width], weight[:, lower:lower + group_width], (((1,), (1,)), ((), ())), preferred_element_type=jnp.float32)
            rounded = lax.optimization_barrier(group_term.astype(jnp.bfloat16))
            summed = summed + rounded.astype(jnp.float32)
        weight_part = lax.dot_general(token_rows, grad_rows, (((0,), (0,)), ((), ())), preferred_element_type=jnp.float32) * grad_scale
        accumulated = accumulated.at[modality].add(weight_part)
        return accumulated, (projected, summed.astype(jnp.bfloat16))

    initial = jnp.zeros((MODALITIES, D, QKV), jnp.float32)
    accumulated, (outputs, input_grads) = lax.scan(loop_step, initial, (token_buffer, grad_buffer, loop_modality))
    projected_rows = outputs.reshape(N_LOOP * slot_count, QKV)[position_index]
    input_grad = input_grads.reshape(N_LOOP * slot_count, D)[position_index]
    return projected_rows, input_grad, accumulated.astype(jnp.bfloat16)
```

```python
import jax
import jax.numpy as jnp
from jax import lax
from jax.experimental import pallas as pl
from jax.experimental.pallas import tpu as pltpu
from jax.sharding import PartitionSpec as P

MESH = pl.DeviceIdType.MESH
F32, BF16 = jnp.float32, jnp.bfloat16
RING = 4
BLOCKS = 8
KINDS = 3
META = 16


def kernel(
    tok_ref, grad_ref, w_ref, dest_ref, kind_ref,
    proj_ref, din_ref, wg_ref,
    xsrc, xbuf, gbuf, wbuf, wtbuf, xt,
    ppart, pr1, pr2, psum, pz,
    dpart, dr1, dr2, dsum, dz, dfin,
    wown, wsend, wrecv,
    local_sem, send_sem, recv_sem,
):
    rows, feat = tok_ref.shape
    cols = grad_ref.shape[1]
    wrows = w_ref.shape[1]
    chip_rows = 2 * wrows
    half = rows // 2
    ext = rows + META

    loop_id = lax.axis_index("loop")
    tp_id = lax.axis_index("tp")
    core = lax.rem(loop_id, 2)
    chip = lax.div(loop_id, 2)
    zh, y = lax.div(chip, RING), lax.rem(chip, RING)
    zl, x = lax.div(tp_id, RING), lax.rem(tp_id, RING)

    def loop_dev(z, r):
        return {"loop": (z * RING + r) * 2 + core, "tp": tp_id}

    def tp_dev(z, r):
        return {"loop": loop_id, "tp": z * RING + r}

    mate = {"loop": chip * 2 + (1 - core), "tp": tp_id}
    flip = {"loop": tp_id * 2 + core, "tp": chip}
    off_diagonal = chip != tp_id

    def right(r):
        return lax.rem(r + 1, RING)

    def left(r):
        return lax.rem(r + RING - 1, RING)

    def across(r):
        return lax.rem(r + 2, RING)

    count = [0]

    def copy(src, dst, device):
        i = count[0]
        count[0] += 1
        return pltpu.make_async_remote_copy(
            src_ref=src, dst_ref=dst, send_sem=send_sem.at[i], recv_sem=recv_sem.at[i],
            device_id=device, device_id_type=MESH,
        )

    barrier = pltpu.get_barrier_semaphore()
    peers = [mate]
    for dev, z, r in ((loop_dev, zh, y), (tp_dev, zl, x)):
        peers += [dev(1 - z, r), dev(z, right(r)), dev(z, left(r))]
    for peer in peers:
        pl.semaphore_signal(barrier, inc=1, device_id=peer, device_id_type=MESH)

    @pl.when(off_diagonal)
    def _():
        pl.semaphore_signal(barrier, inc=1, device_id=flip, device_id_type=MESH)

    load_x = pltpu.make_async_copy(tok_ref, xsrc.at[pl.ds(0, rows)], local_sem.at[0])
    load_x.start()
    load_g = pltpu.make_async_copy(grad_ref, gbuf.at[chip], local_sem.at[1])
    load_g.start()
    load_w = []
    for m in range(KINDS):
        own_rows = pl.ds(m * chip_rows + core * wrows, wrows)
        load_w.append(pltpu.make_async_copy(w_ref.at[m], wbuf.at[own_rows], local_sem.at[2 + m]))
        load_w[-1].start()

    dest = dest_ref[...]
    kind = jnp.full(dest.shape, kind_ref[0], jnp.int32)
    for i in range(1, 2 * BLOCKS):
        kind = jnp.where(dest >= i * (3 * rows // (4 * BLOCKS)), kind_ref[i], kind)
    kind_row = kind.astype(F32)
    top = lax.broadcasted_iota(jnp.int32, (META, rows), 0) == 0
    xsrc[pl.ds(rows, META), pl.ds(0, rows)] = jnp.where(top, kind_row, 0.0).astype(BF16)
    xsrc[pl.ds(rows, META), pl.ds(rows, feat - rows)] = jnp.zeros((META, feat - rows), BF16)

    pl.semaphore_wait(barrier, 7 + jnp.where(off_diagonal, 1, 0))

    class Gather:
        def __init__(self, buf, dev, z, r, length, src):
            own, other = z * RING + r, (1 - z) * RING + r
            low, high = pl.ds(0, half), pl.ds(half, length - half)
            first = buf.at[own] if src is None else src
            self.z = copy(first, buf.at[own], dev(1 - z, r))
            self.own = [copy(first, buf.at[own], dev(z, to)) for to in (right(r), left(r))]
            self.other = [copy(buf.at[other], buf.at[other], dev(z, to)) for to in (right(r), left(r))]
            self.forward = []
            for zz in (z, 1 - z):
                a, b = zz * RING + left(r), zz * RING + right(r)
                self.forward.append([
                    copy(buf.at[a, low], buf.at[a, low], dev(z, right(r))),
                    copy(buf.at[b, high], buf.at[b, high], dev(z, left(r))),
                ])
            self.all = [self.z] + self.own + self.other + self.forward[0] + self.forward[1]

    g = Gather(gbuf, loop_dev, zh, y, rows, grad_ref)
    xg = Gather(xbuf, tp_dev, zl, x, ext, None)
    started = []

    def go(*copies):
        for c in copies:
            c.start()
            started.append(c)

    def arrived(*copies):
        for c in copies:
            c.wait_recv()

    go(g.z, *g.own)

    load_x.wait()
    xflip = copy(xsrc, xbuf.at[chip], flip)
    xsame = pltpu.make_async_copy(xsrc, xbuf.at[chip], local_sem.at[5])

    @pl.when(off_diagonal)
    def _():
        xflip.start()

    @pl.when(jnp.logical_not(off_diagonal))
    def _():
        xsame.start()

    wswap = []
    for m in range(KINDS):
        own_rows = pl.ds(m * chip_rows + core * wrows, wrows)
        wswap.append(copy(w_ref.at[m], wbuf.at[own_rows], mate))
    go(*wswap)

    @pl.when(off_diagonal)
    def _():
        xflip.wait()

    @pl.when(jnp.logical_not(off_diagonal))
    def _():
        xsame.wait()

    go(xg.z, *xg.own)
    arrived(*g.own)
    go(*g.forward[0])
    arrived(g.z)
    go(*g.other)
    arrived(xg.z)
    go(*xg.other)
    arrived(*xg.own)
    go(*xg.forward[0])

    load_g.wait()
    for c in load_w:
        c.wait()
    arrived(*wswap)

    @pl.loop(0, KINDS)
    def _(m):
        at = pl.ds(pl.multiple_of(m * chip_rows, chip_rows), chip_rows)
        wtbuf[:, at] = wbuf[at, :].T

    arrived(*xg.other)
    go(*xg.forward[1])
    arrived(*g.other)
    go(*g.forward[1])
    arrived(*xg.forward[0], *xg.forward[1])

    ones = jnp.ones((META, 128), BF16)

    def kind_columns(b, width):
        row = xbuf[b, pl.ds(rows, META), pl.ds(0, rows)]
        col = lax.dot_general(row, ones, (((0,), (0,)), ((), ())), preferred_element_type=F32)
        return jnp.concatenate([col] * (width // 128), axis=1)

    def project(b):
        tokens = xbuf[b, pl.ds(0, rows), :]
        col = kind_columns(b, feat)
        stacked = jnp.concatenate(
            [jnp.where(col == m, tokens.astype(F32), 0.0).astype(BF16) for m in range(KINDS)], axis=1
        )
        ppart[b] = jnp.dot(stacked, wbuf[...], preferred_element_type=F32).astype(BF16)

    def input_term(b):
        out = jnp.dot(gbuf[b], wtbuf[...], preferred_element_type=F32)
        col = kind_columns(b, feat)
        picked = jnp.where(
            col == 0, out[:, :feat], jnp.where(col == 1, out[:, feat:2 * feat], out[:, 2 * feat:])
        )
        dpart[b] = picked.astype(BF16)

    def transpose_tokens(b):
        tokens_t = xbuf[b, pl.ds(0, rows), :].astype(F32).T
        row = xbuf[b, pl.ds(rows, META), pl.ds(0, rows)].astype(F32)[0:1]
        at = pl.ds(pl.multiple_of(b * rows, rows), rows)
        for m in range(KINDS):
            xt[pl.ds(m * feat, feat), at] = jnp.where(row == m, tokens_t, 0.0).astype(BF16)

    def added(a, *others):
        total = a.astype(F32)
        for o in others:
            total = total + o.astype(F32)
        return total

    class Scatter:
        def __init__(self, part, r1, r2, total, zbuf, dev, z, r):
            low, high = pl.ds(0, half), pl.ds(half, half)
            self.part, self.r1, self.r2, self.total, self.zbuf = part, r1, r2, total, zbuf
            self.low, self.high, self.z, self.r = low, high, z, r
            self.first, self.second = [], []
            for i, zz in enumerate((1 - z, z)):
                far = zz * RING + across(r)
                self.first.append([
                    copy(part.at[far, low], r1.at[i, 0], dev(z, right(r))),
                    copy(part.at[far, high], r1.at[i, 1], dev(z, left(r))),
                ])
                self.second.append([
                    copy(part.at[zz * RING + right(r)], r2.at[i, 0], dev(z, right(r))),
                    copy(part.at[zz * RING + left(r)], r2.at[i, 1], dev(z, left(r))),
                ])
            self.last = copy(total, zbuf, dev(1 - z, r))

        def block(self, i, step):
            zz = (1 - self.z) if i == 0 else self.z
            return zz * RING + lax.rem(self.r + step, RING)

        def relay(self, i):
            arrived(*self.first[i])
            a, b = self.block(i, 1), self.block(i, 3)
            self.part[a, self.low] = added(self.part[a, self.low], self.r1[i, 0]).astype(BF16)
            self.part[b, self.high] = added(self.part[b, self.high], self.r1[i, 1]).astype(BF16)
            go(*self.second[i])

        def close(self, i):
            arrived(*self.second[i])
            return added(self.part[self.block(i, 0)], self.r2[i, 0], self.r2[i, 1])

    ps = Scatter(ppart, pr1, pr2, psum, pz, loop_dev, zh, y)
    ds = Scatter(dpart, dr1, dr2, dsum, dz, tp_dev, zl, x)

    def rest(scatter, i, compute):
        def body(s, carry):
            compute(scatter.block(i, lax.rem(s * 2 + 1, RING + 1)))
            return carry
        lax.fori_loop(0, 3, body, 0)

    project(ps.block(0, 2))
    go(*ps.first[0])
    project(ps.block(1, 2))
    go(*ps.first[1])
    rest(ps, 0, project)
    ps.relay(0)
    rest(ps, 1, project)
    ps.relay(1)

    arrived(*g.forward[0], *g.forward[1])
    input_term(ds.block(0, 2))
    go(*ds.first[0])
    input_term(ds.block(1, 2))
    go(*ds.first[1])
    rest(ds, 0, input_term)
    ds.relay(0)
    rest(ds, 1, input_term)
    ds.relay(1)

    psum[...] = ps.close(0).astype(BF16)
    go(ps.last)

    def tbody(b, carry):
        transpose_tokens(b)
        return carry
    lax.fori_loop(0, BLOCKS, tbody, 0)

    dsum[...] = ds.close(0).astype(BF16)
    go(ds.last)

    gall = gbuf.reshape(BLOCKS * rows, cols)
    wcopies = [copy(wsend.at[m], wrecv.at[m], mate) for m in range(KINDS)]

    def wtile(m, which):
        at = pl.ds(pl.multiple_of(m * chip_rows + which * wrows, wrows), wrows)
        return jnp.dot(xt[at, :], gall[...], preferred_element_type=F32)

    for m in range(KINDS):
        wsend[m] = wtile(m, 1 - core).astype(BF16)
        go(wcopies[m])

    final = ds.close(1)
    arrived(ds.last)
    dfin[...] = (final + dz[...].astype(F32)).astype(BF16)
    dflip = copy(dfin, din_ref, flip)
    dsame = pltpu.make_async_copy(dfin, din_ref, local_sem.at[5])

    @pl.when(off_diagonal)
    def _():
        dflip.start()

    @pl.when(jnp.logical_not(off_diagonal))
    def _():
        dsame.start()

    def wbody(m, carry):
        wown[m] = wtile(m, core)
        return carry
    lax.fori_loop(0, KINDS, wbody, 0)

    scale = float(2 * BLOCKS * rows) ** -0.5
    for m in range(KINDS):
        arrived(wcopies[m])
        wg_ref[m] = ((wown[m] + wrecv[m].astype(F32)) * scale).astype(BF16)

    final = ps.close(1)
    arrived(ps.last)
    proj_ref[...] = (final + pz[...].astype(F32)).astype(BF16)

    @pl.when(off_diagonal)
    def _():
        dflip.wait()

    @pl.when(jnp.logical_not(off_diagonal))
    def _():
        dsame.wait()

    for c in started:
        c.wait_send()


def per_device(tokens, out_grad, qkv_weight, dest_row, loop_modality):
    rows, feat = tokens.shape
    cols = out_grad.shape[1]
    kinds, wrows, _ = qkv_weight.shape
    half = rows // 2
    any_spec = pl.BlockSpec(memory_space=pl.ANY)
    vmem = pl.BlockSpec(memory_space=pltpu.VMEM)
    deep = kinds * 2 * wrows

    def scatter_buffers(width):
        return [
            pltpu.VMEM((BLOCKS, rows, width), BF16),
            pltpu.VMEM((2, 2, half, width), BF16),
            pltpu.VMEM((2, 2, rows, width), BF16),
            pltpu.VMEM((rows, width), BF16),
            pltpu.VMEM((rows, width), BF16),
        ]

    return pl.pallas_call(
        kernel,
        out_shape=(
            jax.ShapeDtypeStruct((rows, cols), BF16),
            jax.ShapeDtypeStruct((rows, feat), BF16),
            jax.ShapeDtypeStruct(qkv_weight.shape, BF16),
        ),
        in_specs=[any_spec, any_spec, any_spec, vmem, pl.BlockSpec(memory_space=pltpu.SMEM)],
        out_specs=(vmem, vmem, vmem),
        scratch_shapes=[
            pltpu.VMEM((rows + META, feat), BF16),
            pltpu.VMEM((BLOCKS, rows + META, feat), BF16),
            pltpu.VMEM((BLOCKS, rows, cols), BF16),
            pltpu.VMEM((deep, cols), BF16),
            pltpu.VMEM((cols, deep), BF16),
            pltpu.VMEM((deep, BLOCKS * rows), BF16),
            *scatter_buffers(cols),
            *scatter_buffers(feat),
            pltpu.VMEM((rows, feat), BF16),
            pltpu.VMEM((kinds, wrows, cols), F32),
            pltpu.VMEM((kinds, wrows, cols), BF16),
            pltpu.VMEM((kinds, wrows, cols), BF16),
            pltpu.SemaphoreType.DMA((6,)),
            pltpu.SemaphoreType.DMA((64,)),
            pltpu.SemaphoreType.DMA((64,)),
        ],
        compiler_params=pltpu.CompilerParams(
            collective_id=0, has_side_effects=True, vmem_limit_bytes=60 * 1024 * 1024
        ),
        name="stationary",
    )(tokens, out_grad, qkv_weight, dest_row.reshape(1, rows), loop_modality)


def solution(mesh):
    placed = (P("loop", "tp"), P("loop", "tp"), P(None, "loop", "tp"), P("loop"), P())
    return jax.shard_map(
        per_device,
        mesh=mesh,
        in_specs=placed,
        out_specs=(P("loop", "tp"), P("loop", "tp"), P(None, "loop", "tp")),
        check_vma=False,
    )
```

```python
import jax
import jax.numpy as jnp
from jax import lax
from jax.experimental import pallas as pl
from jax.experimental.pallas import tpu as pltpu
from jax.sharding import PartitionSpec as P

MESH = pl.DeviceIdType.MESH
F32, BF16 = jnp.float32, jnp.bfloat16
RING = 4
BLOCKS = 8
KINDS = 3
META = 16


def kernel(
    tok_ref, grad_ref, w_ref, dest_ref, kind_ref,
    proj_ref, din_ref, wg_ref,
    kinds, xbuf, gbuf, wbuf, wtbuf, xt,
    ppart, pa, pb, pc, psum, pz,
    dpart, dr1, dr2, dsum, dz, dfin, dmid,
    wown, wsend, wrecv,
    local_sem, send_sem, recv_sem,
):
    rows, feat = tok_ref.shape
    cols = grad_ref.shape[1]
    wrows = w_ref.shape[1]
    chip_rows = 2 * wrows
    half = rows // 2
    low, high = pl.ds(0, half), pl.ds(half, half)

    loop_id = lax.axis_index("loop")
    tp_id = lax.axis_index("tp")
    core = lax.rem(loop_id, 2)
    chip = lax.div(loop_id, 2)
    zh, y = lax.div(chip, RING), lax.rem(chip, RING)
    zl, x = lax.div(tp_id, RING), lax.rem(tp_id, RING)

    def at(a, b):
        return {"loop": a * 2 + core, "tp": b}

    def loop_dev(z, r):
        return at(z * RING + r, tp_id)

    def tp_dev(z, r):
        return at(chip, z * RING + r)

    mate = {"loop": chip * 2 + (1 - core), "tp": tp_id}
    plus, minus = lax.rem(x + y, RING), lax.rem(x - y + RING, RING)
    flip_to = at(zl * RING + x, zh * RING + plus)
    flip_from = at(zl * RING + minus, zh * RING + y)
    flip_moves = jnp.logical_not((zh == zl) & (x == y) & (y == 0))
    turn = at(zl * RING + minus, zh * RING + x)
    turn_moves = jnp.logical_not((zh == zl) & (minus == y))
    slide_to = at(chip, zl * RING + minus)
    slide_from = at(chip, zl * RING + plus)
    slide_moves = y != 0

    def slot_of(b):
        return lax.div(b, RING) * RING + lax.rem(lax.rem(b, RING) + y, RING)

    def block_of(s):
        return lax.div(s, RING) * RING + lax.rem(lax.rem(s, RING) - y + RING, RING)

    def right(r):
        return lax.rem(r + 1, RING)

    def left(r):
        return lax.rem(r + RING - 1, RING)

    def across(r):
        return lax.rem(r + 2, RING)

    count = [0]
    started = []

    def copy(src, dst, device):
        i = count[0]
        count[0] += 1
        return pltpu.make_async_remote_copy(
            src_ref=src, dst_ref=dst, send_sem=send_sem.at[i], recv_sem=recv_sem.at[i],
            device_id=device, device_id_type=MESH,
        )

    def go(*copies):
        for c in copies:
            c.start()
            started.append(c)

    def arrived(*copies):
        for c in copies:
            c.wait_recv()

    class Move:
        def __init__(self, src, dst, device, moves, sem):
            self.remote = copy(src, dst, device)
            self.local = pltpu.make_async_copy(src, dst, local_sem.at[sem])
            self.moves = moves

        def start(self):
            pl.when(self.moves)(self.remote.start)
            pl.when(jnp.logical_not(self.moves))(self.local.start)

        def arrived(self):
            pl.when(self.moves)(self.remote.wait_recv)
            pl.when(jnp.logical_not(self.moves))(self.local.wait)

        def sent(self):
            pl.when(self.moves)(self.remote.wait_send)

    barrier = pltpu.get_barrier_semaphore()

    def greet(device):
        pl.semaphore_signal(barrier, inc=1, device_id=device, device_id_type=MESH)

    loop_peers = []
    for i in range(1, BLOCKS):
        z = lax.rem(zh + i // RING, 2)
        loop_peers.append(loop_dev(z, lax.rem(y + i % RING, RING)))
    for peer in loop_peers + [mate, tp_dev(1 - zl, x), tp_dev(zl, right(x)), tp_dev(zl, left(x))]:
        greet(peer)

    @pl.when(flip_moves)
    def _():
        greet(flip_to)
        greet(flip_from)

    @pl.when(turn_moves)
    def _():
        greet(turn)

    @pl.when(slide_moves)
    def _():
        greet(slide_to)
        greet(slide_from)

    load_g = pltpu.make_async_copy(grad_ref, gbuf.at[chip], local_sem.at[1])
    load_g.start()
    load_w = []
    for m in range(KINDS):
        own_rows = pl.ds(m * chip_rows + core * wrows, wrows)
        load_w.append(pltpu.make_async_copy(w_ref.at[m], wbuf.at[own_rows], local_sem.at[2 + m]))
        load_w[-1].start()

    dest = dest_ref[...]
    kind = jnp.full(dest.shape, kind_ref[0], jnp.int32)
    for i in range(1, 2 * BLOCKS):
        kind = jnp.where(dest >= i * (3 * rows // (4 * BLOCKS)), kind_ref[i], kind)
    top = lax.broadcasted_iota(jnp.int32, (META, rows), 0) == 0
    kinds[chip] = jnp.where(top, kind.astype(F32), 0.0).astype(BF16)

    expected = len(loop_peers) + 4 + jnp.where(flip_moves, 2, 0)
    pl.semaphore_wait(
        barrier, expected + jnp.where(turn_moves, 1, 0) + jnp.where(slide_moves, 2, 0)
    )

    flips = [
        Move(tok_ref.at[part], xbuf.at[zh * RING + plus, part], flip_to, flip_moves, 5 + i)
        for i, part in enumerate((low, high))
    ]
    flips[0].start()

    class Gather:
        def __init__(self, buf, dev, z, r, src, balanced):
            own, other = z * RING + r, (1 - z) * RING + r
            first = buf.at[own] if src is None else src
            to_right, to_left, over = dev(z, right(r)), dev(z, left(r)), dev(1 - z, r)
            self.z = [copy(first.at[p], buf.at[own, p], over) for p in (low, high)]
            self.own_right = [copy(first.at[p], buf.at[own, p], to_right) for p in (low, high)]
            self.own_left = [copy(first.at[p], buf.at[own, p], to_left) for p in (low, high)]
            self.forward, self.cross = [], []
            for zz in (z, 1 - z):
                a, b = buf.at[zz * RING + left(r), low], buf.at[zz * RING + right(r), high]
                self.forward.append([copy(a, a, to_right), copy(b, b, to_left)])
                if balanced and not self.cross:
                    self.cross = [copy(a, a, over), copy(b, b, over)]
            a, b = (buf.at[other, high], buf.at[other, low]) if balanced else (buf.at[other],) * 2
            self.other = [copy(a, a, to_right), copy(b, b, to_left)]

    g = Gather(gbuf, loop_dev, zh, y, grad_ref, True)
    xg = Gather(xbuf, tp_dev, zl, x, None, False)
    tell = [copy(kinds.at[chip], kinds.at[chip], peer) for peer in loop_peers]
    wswap = []
    for m in range(KINDS):
        own_rows = pl.ds(m * chip_rows + core * wrows, wrows)
        wswap.append(copy(w_ref.at[m], wbuf.at[own_rows], mate))

    go(*tell)
    go(g.own_right[0], g.own_left[1], g.z[0])
    flips[1].start()
    go(g.own_right[1], g.own_left[0], g.z[1])
    go(*wswap)

    ones = jnp.ones((META, 128), BF16)

    def kind_columns(b, width):
        col = lax.dot_general(
            kinds[b], ones, (((0,), (0,)), ((), ())), preferred_element_type=F32
        )
        return jnp.concatenate([col] * (width // 128), axis=1)

    def project(s):
        b = block_of(s)
        tokens = xbuf[s].astype(F32)
        col = kind_columns(b, feat)
        stacked = jnp.concatenate(
            [jnp.where(col == m, tokens, 0.0).astype(BF16) for m in range(KINDS)], axis=1
        )
        ppart[b] = jnp.dot(stacked, wbuf[...], preferred_element_type=F32).astype(BF16)

    def input_term(b):
        out = jnp.dot(gbuf[b], wtbuf[...], preferred_element_type=F32)
        col = kind_columns(b, feat)
        picked = jnp.where(
            col == 0, out[:, :feat], jnp.where(col == 1, out[:, feat:2 * feat], out[:, 2 * feat:])
        )
        dpart[slot_of(b)] = picked.astype(BF16)

    def each(compute, first, second):
        def body(i, carry):
            compute(jnp.where(i == 0, first, second))
            return carry
        lax.fori_loop(0, 2, body, 0)

    def near(z, r):
        return z * RING + right(r), z * RING + left(r)

    for c in load_w:
        c.wait()
    arrived(*wswap)
    load_g.wait()

    def turn_weights(m, carry):
        span = pl.ds(pl.multiple_of(m * chip_rows, chip_rows), chip_rows)
        wtbuf[:, span] = wbuf[span, :].T
        return carry
    lax.fori_loop(0, KINDS, turn_weights, 0)

    flips[0].arrived()
    go(xg.own_right[0], xg.own_left[0], xg.z[0])
    arrived(g.own_right[0], g.own_left[1])
    go(*g.forward[0], *g.cross)
    flips[1].arrived()
    go(xg.own_left[1], xg.own_right[1], xg.z[1])
    arrived(*tell)
    input_term(chip)
    project(tp_id)

    arrived(*g.z)
    go(*g.other)
    arrived(xg.own_right[0], xg.own_left[1])
    go(*xg.forward[0])
    arrived(*xg.z)
    go(*xg.other)
    arrived(g.own_right[1], g.own_left[0])
    each(input_term, *near(zh, y))
    arrived(xg.own_right[1], xg.own_left[0])
    each(project, *near(zl, x))
    arrived(*g.cross)
    go(*g.forward[1])
    arrived(*g.forward[0])
    each(input_term, (1 - zh) * RING + y, zh * RING + across(y))
    arrived(*xg.other)
    go(*xg.forward[1])
    arrived(*g.other)
    each(input_term, *near(1 - zh, y))
    each(project, *near(1 - zl, x))
    arrived(*xg.forward[0])
    each(project, (1 - zl) * RING + x, zl * RING + across(x))

    def added(a, *others):
        total = a.astype(F32)
        for o in others:
            total = total + o.astype(F32)
        return total

    class Scatter:
        def __init__(self, part, r1, r2, total, zbuf, dev, z, r):
            self.part, self.r1, self.r2, self.total, self.zbuf = part, r1, r2, total, zbuf
            self.z, self.r = z, r
            self.first, self.second = [], []
            for i, zz in enumerate((1 - z, z)):
                far = zz * RING + across(r)
                self.first.append([
                    copy(part.at[far, low], r1.at[i, 0], dev(z, right(r))),
                    copy(part.at[far, high], r1.at[i, 1], dev(z, left(r))),
                ])
                self.second.append([
                    copy(part.at[zz * RING + right(r)], r2.at[i, 0], dev(z, right(r))),
                    copy(part.at[zz * RING + left(r)], r2.at[i, 1], dev(z, left(r))),
                ])
            self.last = copy(total, zbuf, dev(1 - z, r))

        def block(self, i, step):
            zz = (1 - self.z) if i == 0 else self.z
            return zz * RING + lax.rem(self.r + step, RING)

        def relay(self, i):
            arrived(*self.first[i])
            a, b = self.block(i, 1), self.block(i, 3)
            self.part[a, low] = added(self.part[a, low], self.r1[i, 0]).astype(BF16)
            self.part[b, high] = added(self.part[b, high], self.r1[i, 1]).astype(BF16)
            go(*self.second[i])

        def close(self, i):
            arrived(*self.second[i])
            return added(self.part[self.block(i, 0)], self.r2[i, 0], self.r2[i, 1])

    class Balanced:
        def __init__(self, part, ra, rb, rc, total, zbuf, dev, z, r):
            o = 1 - z
            self.part, self.ra, self.rb, self.rc, self.total, self.zbuf = part, ra, rb, rc, total, zbuf
            self.to = [(o if i == 0 else z) * RING for i in range(2)]
            self.l, self.r_, self.r = left(r), right(r), r
            far = across(r)
            to_left, to_right, over = dev(z, left(r)), dev(z, right(r)), dev(o, r)
            oo, zz = o * RING, z * RING
            self.a = [
                copy(part.at[oo + far, low], ra.at[0], to_left),
                copy(part.at[oo + far, high], ra.at[1], to_right),
                copy(part.at[oo + self.l, high], ra.at[2], to_left),
                copy(part.at[oo + self.r_, low], ra.at[3], to_right),
                copy(part.at[zz + far, low], ra.at[4], to_left),
                copy(part.at[zz + far, high], ra.at[5], to_right),
            ]
            self.b = [
                copy(part.at[oo + self.l, low], rb.at[0], over),
                copy(part.at[oo + self.r_, high], rb.at[1], over),
            ]
            self.last = copy(total, zbuf, over)
            self.c = [
                copy(part.at[zz + self.l], rc.at[0], to_left),
                copy(part.at[zz + self.r_], rc.at[1], to_right),
            ]
            self.oo, self.zz = oo, zz

        def relay(self):
            part, ra = self.part, self.ra
            a, b = self.oo + self.l, self.oo + self.r_
            arrived(*self.a[:2])
            part[a, low] = added(part[a, low], ra[0]).astype(BF16)
            part[b, high] = added(part[b, high], ra[1]).astype(BF16)
            go(*self.b)

        def middle(self):
            part, ra = self.part, self.ra
            own = self.oo + self.r
            arrived(*self.a[2:4])
            self.total[low] = added(part[own, low], ra[3]).astype(BF16)
            self.total[high] = added(part[own, high], ra[2]).astype(BF16)
            go(self.last)

        def near(self):
            part, ra, rb = self.part, self.ra, self.rb
            a, b = self.zz + self.l, self.zz + self.r_
            arrived(*self.a[4:], *self.b)
            part[a, low] = added(part[a, low], ra[4], rb[0]).astype(BF16)
            part[b, high] = added(part[b, high], ra[5], rb[1]).astype(BF16)
            go(*self.c)

        def close(self):
            arrived(*self.c, self.last)
            return added(
                self.part[self.zz + self.r], self.rc[0], self.rc[1], self.zbuf[...]
            )

    ps = Balanced(ppart, pa, pb, pc, psum, pz, loop_dev, zh, y)
    ds = Scatter(dpart, dr1, dr2, dsum, dz, tp_dev, zl, x)

    arrived(*g.forward[1])
    input_term((1 - zh) * RING + across(y))
    go(*ds.first[0], *ds.first[1])
    arrived(*xg.forward[1])
    project((1 - zl) * RING + across(x))
    go(*ps.a)

    def transpose_tokens(s, carry):
        b = block_of(s)
        tokens_t = xbuf[s].astype(F32).T
        row = kinds[b].astype(F32)[0:1]
        span = pl.ds(pl.multiple_of(b * rows, rows), rows)
        for m in range(KINDS):
            xt[pl.ds(m * feat, feat), span] = jnp.where(row == m, tokens_t, 0.0).astype(BF16)
        return carry
    lax.fori_loop(0, BLOCKS, transpose_tokens, 0)

    ds.relay(0)
    ps.relay()

    gall = gbuf.reshape(BLOCKS * rows, cols)
    wcopies = [copy(wsend.at[m], wrecv.at[m], mate) for m in range(KINDS)]

    def wtile(m, which):
        span = pl.ds(pl.multiple_of(m * chip_rows + which * wrows, wrows), wrows)
        return jnp.dot(xt[span, :], gall[...], preferred_element_type=F32)

    def wside(m, carry):
        wsend[m] = wtile(m, 1 - core).astype(BF16)
        return carry
    lax.fori_loop(0, KINDS, wside, 0)
    go(*wcopies)
    ds.relay(1)
    ps.middle()

    def wkeep(m, carry):
        wown[m] = wtile(m, core)
        return carry
    lax.fori_loop(0, KINDS, wkeep, 0)

    dsum[...] = ds.close(0).astype(BF16)
    go(ds.last)
    ps.near()

    scale = float(2 * BLOCKS * rows) ** -0.5
    for m in range(KINDS):
        arrived(wcopies[m])
        wg_ref[m] = ((wown[m] + wrecv[m].astype(F32)) * scale).astype(BF16)

    final = ds.close(1)
    arrived(ds.last)
    dfin[...] = (final + dz[...].astype(F32)).astype(BF16)
    turns = [
        Move(dfin.at[part], dmid.at[part], turn, turn_moves, 5 + i)
        for i, part in enumerate((low, high))
    ]
    slides = [
        Move(dmid.at[part], din_ref.at[part], slide_to, slide_moves, 7 + i)
        for i, part in enumerate((low, high))
    ]
    for t in turns:
        t.start()
    for t, s in zip(turns, slides):
        t.arrived()
        s.start()

    proj_ref[...] = ps.close().astype(BF16)
    for s in slides:
        s.arrived()
    for move in flips + turns + slides:
        move.sent()
    for c in started:
        c.wait_send()


def per_device(tokens, out_grad, qkv_weight, dest_row, loop_modality):
    rows, feat = tokens.shape
    cols = out_grad.shape[1]
    kinds, wrows, _ = qkv_weight.shape
    half = rows // 2
    any_spec = pl.BlockSpec(memory_space=pl.ANY)
    vmem = pl.BlockSpec(memory_space=pltpu.VMEM)
    deep = kinds * 2 * wrows

    return pl.pallas_call(
        kernel,
        out_shape=(
            jax.ShapeDtypeStruct((rows, cols), BF16),
            jax.ShapeDtypeStruct((rows, feat), BF16),
            jax.ShapeDtypeStruct(qkv_weight.shape, BF16),
        ),
        in_specs=[any_spec, any_spec, any_spec, vmem, pl.BlockSpec(memory_space=pltpu.SMEM)],
        out_specs=(vmem, vmem, vmem),
        scratch_shapes=[
            pltpu.VMEM((BLOCKS, META, rows), BF16),
            pltpu.VMEM((BLOCKS, rows, feat), BF16),
            pltpu.VMEM((BLOCKS, rows, cols), BF16),
            pltpu.VMEM((deep, cols), BF16),
            pltpu.VMEM((cols, deep), BF16),
            pltpu.VMEM((deep, BLOCKS * rows), BF16),
            pltpu.VMEM((BLOCKS, rows, cols), BF16),
            pltpu.VMEM((6, half, cols), BF16),
            pltpu.VMEM((2, half, cols), BF16),
            pltpu.VMEM((2, rows, cols), BF16),
            pltpu.VMEM((rows, cols), BF16),
            pltpu.VMEM((rows, cols), BF16),
            pltpu.VMEM((BLOCKS, rows, feat), BF16),
            pltpu.VMEM((2, 2, half, feat), BF16),
            pltpu.VMEM((2, 2, rows, feat), BF16),
            pltpu.VMEM((rows, feat), BF16),
            pltpu.VMEM((rows, feat), BF16),
            pltpu.VMEM((rows, feat), BF16),
            pltpu.VMEM((rows, feat), BF16),
            pltpu.VMEM((kinds, wrows, cols), F32),
            pltpu.VMEM((kinds, wrows, cols), BF16),
            pltpu.VMEM((kinds, wrows, cols), BF16),
            pltpu.SemaphoreType.DMA((9,)),
            pltpu.SemaphoreType.DMA((80,)),
            pltpu.SemaphoreType.DMA((80,)),
        ],
        compiler_params=pltpu.CompilerParams(
            collective_id=0, has_side_effects=True, vmem_limit_bytes=60 * 1024 * 1024
        ),
        name="stationary",
    )(tokens, out_grad, qkv_weight, dest_row.reshape(1, rows), loop_modality)


def solution(mesh):
    placed = (P("loop", "tp"), P("loop", "tp"), P(None, "loop", "tp"), P("loop"), P())
    return jax.shard_map(
        per_device,
        mesh=mesh,
        in_specs=placed,
        out_specs=(P("loop", "tp"), P("loop", "tp"), P(None, "loop", "tp")),
        check_vma=False,
    )
```

```python
import jax
import jax.numpy as jnp
from jax import lax
from jax.experimental import pallas as pl
from jax.experimental.pallas import tpu as pltpu
from jax.sharding import PartitionSpec as P

MESH = pl.DeviceIdType.MESH
F32, BF16 = jnp.float32, jnp.bfloat16
RING = 4
BLOCKS = 8
KINDS = 3
META = 16


def kernel(
    tok_ref, grad_ref, w_ref, dest_ref, kind_ref,
    proj_ref, din_ref, wg_ref,
    kinds, xbuf, gbuf, wbuf, wtbuf, xt,
    ppart, pa, pb, pc, psum, pz,
    dpart, dr1, dr2, dsum, dz, dfin, dmid,
    wown, wsend, wrecv,
    local_sem, send_sem, recv_sem,
):
    rows, feat = tok_ref.shape
    cols = grad_ref.shape[1]
    wrows = w_ref.shape[1]
    chip_rows = 2 * wrows
    half = rows // 2
    low, high = pl.ds(0, half), pl.ds(half, half)

    loop_id = lax.axis_index("loop")
    tp_id = lax.axis_index("tp")
    core = lax.rem(loop_id, 2)
    chip = lax.div(loop_id, 2)
    zh, y = lax.div(chip, RING), lax.rem(chip, RING)
    zl, x = lax.div(tp_id, RING), lax.rem(tp_id, RING)

    def at(a, b):
        return {"loop": a * 2 + core, "tp": b}

    def loop_dev(z, r):
        return at(z * RING + r, tp_id)

    def tp_dev(z, r):
        return at(chip, z * RING + r)

    mate = {"loop": chip * 2 + (1 - core), "tp": tp_id}
    plus, minus = lax.rem(x + y, RING), lax.rem(x - y + RING, RING)
    flip_to = at(zl * RING + x, zh * RING + plus)
    flip_from = at(zl * RING + minus, zh * RING + y)
    flip_moves = jnp.logical_not((zh == zl) & (x == y) & (y == 0))
    turn = at(zl * RING + minus, zh * RING + x)
    turn_moves = jnp.logical_not((zh == zl) & (minus == y))
    slide_to = at(chip, zl * RING + minus)
    slide_from = at(chip, zl * RING + plus)
    slide_moves = y != 0

    def slot_of(b):
        return lax.div(b, RING) * RING + lax.rem(lax.rem(b, RING) + y, RING)

    def block_of(s):
        return lax.div(s, RING) * RING + lax.rem(lax.rem(s, RING) - y + RING, RING)

    def right(r):
        return lax.rem(r + 1, RING)

    def left(r):
        return lax.rem(r + RING - 1, RING)

    def across(r):
        return lax.rem(r + 2, RING)

    count = [0]
    started = []

    def copy(src, dst, device):
        i = count[0]
        count[0] += 1
        return pltpu.make_async_remote_copy(
            src_ref=src, dst_ref=dst, send_sem=send_sem.at[i], recv_sem=recv_sem.at[i],
            device_id=device, device_id_type=MESH,
        )

    def go(*copies):
        for c in copies:
            c.start()
            started.append(c)

    def arrived(*copies):
        for c in copies:
            c.wait_recv()

    class Move:
        def __init__(self, src, dst, device, moves, sem):
            self.remote = copy(src, dst, device)
            self.local = pltpu.make_async_copy(src, dst, local_sem.at[sem])
            self.moves = moves

        def start(self):
            pl.when(self.moves)(self.remote.start)
            pl.when(jnp.logical_not(self.moves))(self.local.start)

        def arrived(self):
            pl.when(self.moves)(self.remote.wait_recv)
            pl.when(jnp.logical_not(self.moves))(self.local.wait)

        def sent(self):
            pl.when(self.moves)(self.remote.wait_send)

    barrier = pltpu.get_barrier_semaphore()

    def greet(device):
        pl.semaphore_signal(barrier, inc=1, device_id=device, device_id_type=MESH)

    loop_peers = []
    for i in range(1, BLOCKS):
        z = lax.rem(zh + i // RING, 2)
        loop_peers.append(loop_dev(z, lax.rem(y + i % RING, RING)))
    for peer in loop_peers + [mate, tp_dev(1 - zl, x), tp_dev(zl, right(x)), tp_dev(zl, left(x))]:
        greet(peer)

    @pl.when(flip_moves)
    def _():
        greet(flip_to)
        greet(flip_from)

    @pl.when(turn_moves)
    def _():
        greet(turn)

    @pl.when(slide_moves)
    def _():
        greet(slide_to)
        greet(slide_from)

    load_g = pltpu.make_async_copy(grad_ref, gbuf.at[chip], local_sem.at[1])
    load_g.start()
    load_w = []
    for m in range(KINDS):
        own_rows = pl.ds(m * chip_rows + core * wrows, wrows)
        load_w.append(pltpu.make_async_copy(w_ref.at[m], wbuf.at[own_rows], local_sem.at[2 + m]))
        load_w[-1].start()

    dest = dest_ref[...]
    kind = jnp.full(dest.shape, kind_ref[0], jnp.int32)
    for i in range(1, 2 * BLOCKS):
        kind = jnp.where(dest >= i * (3 * rows // (4 * BLOCKS)), kind_ref[i], kind)
    top = lax.broadcasted_iota(jnp.int32, (META, rows), 0) == 0
    kinds[chip] = jnp.where(top, kind.astype(F32), 0.0).astype(BF16)

    expected = len(loop_peers) + 4 + jnp.where(flip_moves, 2, 0)
    pl.semaphore_wait(
        barrier, expected + jnp.where(turn_moves, 1, 0) + jnp.where(slide_moves, 2, 0)
    )

    flips = [
        Move(tok_ref.at[part], xbuf.at[zh * RING + plus, part], flip_to, flip_moves, 5 + i)
        for i, part in enumerate((low, high))
    ]
    flips[0].start()

    class Gather:
        def __init__(self, buf, dev, z, r, src, balanced):
            own, other = z * RING + r, (1 - z) * RING + r
            first = buf.at[own] if src is None else src
            to_right, to_left, over = dev(z, right(r)), dev(z, left(r)), dev(1 - z, r)
            self.z = [copy(first.at[p], buf.at[own, p], over) for p in (low, high)]
            self.own_right = [copy(first.at[p], buf.at[own, p], to_right) for p in (low, high)]
            self.own_left = [copy(first.at[p], buf.at[own, p], to_left) for p in (low, high)]
            self.forward, self.cross = [], []
            for zz in (z, 1 - z):
                a, b = buf.at[zz * RING + left(r), low], buf.at[zz * RING + right(r), high]
                self.forward.append([copy(a, a, to_right), copy(b, b, to_left)])
                if balanced and not self.cross:
                    self.cross = [copy(a, a, over), copy(b, b, over)]
            a, b = (buf.at[other, high], buf.at[other, low]) if balanced else (buf.at[other],) * 2
            self.other = [copy(a, a, to_right), copy(b, b, to_left)]

    g = Gather(gbuf, loop_dev, zh, y, grad_ref, True)
    xg = Gather(xbuf, tp_dev, zl, x, None, False)
    tell = [copy(kinds.at[chip], kinds.at[chip], peer) for peer in loop_peers]
    wswap = []
    for m in range(KINDS):
        own_rows = pl.ds(m * chip_rows + core * wrows, wrows)
        wswap.append(copy(w_ref.at[m], wbuf.at[own_rows], mate))

    flips[1].start()
    go(*tell)
    go(*wswap)
    go(*g.z, g.own_right[0], g.own_left[1], g.own_right[1], g.own_left[0])

    ones = jnp.ones((META, 128), BF16)

    def kind_columns(b, width):
        col = lax.dot_general(
            kinds[b], ones, (((0,), (0,)), ((), ())), preferred_element_type=F32
        )
        return jnp.concatenate([col] * (width // 128), axis=1)

    def project(s):
        b = block_of(s)
        tokens = xbuf[s].astype(F32)
        col = kind_columns(b, feat)
        stacked = jnp.concatenate(
            [jnp.where(col == m, tokens, 0.0).astype(BF16) for m in range(KINDS)], axis=1
        )
        ppart[b] = jnp.dot(stacked, wbuf[...], preferred_element_type=F32).astype(BF16)

    def input_term(b):
        out = jnp.dot(gbuf[b], wtbuf[...], preferred_element_type=F32)
        col = kind_columns(b, feat)
        picked = jnp.where(
            col == 0, out[:, :feat], jnp.where(col == 1, out[:, feat:2 * feat], out[:, 2 * feat:])
        )
        dpart[slot_of(b)] = picked.astype(BF16)

    def each(compute, first, second):
        def body(i, carry):
            compute(jnp.where(i == 0, first, second))
            return carry
        lax.fori_loop(0, 2, body, 0)

    def near(z, r):
        return z * RING + right(r), z * RING + left(r)

    for c in load_w:
        c.wait()
    arrived(*wswap)
    load_g.wait()

    def turn_weights(m, carry):
        span = pl.ds(pl.multiple_of(m * chip_rows, chip_rows), chip_rows)
        wtbuf[:, span] = wbuf[span, :].T
        return carry
    lax.fori_loop(0, KINDS, turn_weights, 0)

    flips[0].arrived()
    go(xg.z[0], xg.own_right[0], xg.own_left[0])
    flips[1].arrived()
    go(xg.z[1], xg.own_left[1], xg.own_right[1])
    arrived(g.own_right[0], g.own_left[1])
    go(*g.forward[0], *g.cross)
    arrived(*g.z)
    go(*g.other)
    arrived(*tell)
    input_term(chip)
    project(tp_id)

    arrived(xg.own_right[0], xg.own_left[1])
    go(*xg.forward[0])
    arrived(*xg.z)
    go(*xg.other)
    arrived(g.own_right[1], g.own_left[0])
    each(input_term, *near(zh, y))
    arrived(xg.own_right[1], xg.own_left[0])
    each(project, *near(zl, x))
    arrived(*g.forward[0])
    each(input_term, (1 - zh) * RING + y, zh * RING + across(y))
    arrived(*g.cross)
    go(*g.forward[1])
    arrived(*xg.other)
    go(*xg.forward[1])
    arrived(*g.other)
    each(input_term, *near(1 - zh, y))
    each(project, *near(1 - zl, x))
    arrived(*xg.forward[0])
    each(project, (1 - zl) * RING + x, zl * RING + across(x))

    def added(a, *others):
        total = a.astype(F32)
        for o in others:
            total = total + o.astype(F32)
        return total

    class Scatter:
        def __init__(self, part, r1, r2, total, zbuf, dev, z, r):
            self.part, self.r1, self.r2, self.total, self.zbuf = part, r1, r2, total, zbuf
            self.z, self.r = z, r
            self.first, self.second = [], []
            for i, zz in enumerate((1 - z, z)):
                far = zz * RING + across(r)
                self.first.append([
                    copy(part.at[far, low], r1.at[i, 0], dev(z, right(r))),
                    copy(part.at[far, high], r1.at[i, 1], dev(z, left(r))),
                ])
                self.second.append([
                    copy(part.at[zz * RING + right(r)], r2.at[i, 0], dev(z, right(r))),
                    copy(part.at[zz * RING + left(r)], r2.at[i, 1], dev(z, left(r))),
                ])
            self.last = copy(total, zbuf, dev(1 - z, r))

        def block(self, i, step):
            zz = (1 - self.z) if i == 0 else self.z
            return zz * RING + lax.rem(self.r + step, RING)

        def relay(self, i):
            arrived(*self.first[i])
            a, b = self.block(i, 1), self.block(i, 3)
            self.part[a, low] = added(self.part[a, low], self.r1[i, 0]).astype(BF16)
            self.part[b, high] = added(self.part[b, high], self.r1[i, 1]).astype(BF16)
            go(*self.second[i])

        def close(self, i):
            arrived(*self.second[i])
            return added(self.part[self.block(i, 0)], self.r2[i, 0], self.r2[i, 1])

    class Balanced:
        def __init__(self, part, ra, rb, rc, total, zbuf, dev, z, r):
            o = 1 - z
            self.part, self.ra, self.rb, self.rc, self.total, self.zbuf = part, ra, rb, rc, total, zbuf
            self.to = [(o if i == 0 else z) * RING for i in range(2)]
            self.l, self.r_, self.r = left(r), right(r), r
            far = across(r)
            to_left, to_right, over = dev(z, left(r)), dev(z, right(r)), dev(o, r)
            oo, zz = o * RING, z * RING
            self.a = [
                copy(part.at[oo + far, low], ra.at[0], to_left),
                copy(part.at[oo + far, high], ra.at[1], to_right),
                copy(part.at[oo + self.l, high], ra.at[2], to_left),
                copy(part.at[oo + self.r_, low], ra.at[3], to_right),
                copy(part.at[zz + far, low], ra.at[4], to_left),
                copy(part.at[zz + far, high], ra.at[5], to_right),
            ]
            self.b = [
                copy(part.at[oo + self.l, low], rb.at[0], over),
                copy(part.at[oo + self.r_, high], rb.at[1], over),
            ]
            self.last = copy(total, zbuf, over)
            self.c = [
                copy(part.at[zz + self.l], rc.at[0], to_left),
                copy(part.at[zz + self.r_], rc.at[1], to_right),
            ]
            self.oo, self.zz = oo, zz

        def relay(self):
            part, ra = self.part, self.ra
            a, b = self.oo + self.l, self.oo + self.r_
            arrived(*self.a[:2])
            part[a, low] = added(part[a, low], ra[0]).astype(BF16)
            part[b, high] = added(part[b, high], ra[1]).astype(BF16)
            go(*self.b)

        def middle(self):
            part, ra = self.part, self.ra
            own = self.oo + self.r
            arrived(*self.a[2:4])
            self.total[low] = added(part[own, low], ra[3]).astype(BF16)
            self.total[high] = added(part[own, high], ra[2]).astype(BF16)
            go(self.last)

        def near(self):
            part, ra, rb = self.part, self.ra, self.rb
            a, b = self.zz + self.l, self.zz + self.r_
            arrived(*self.a[4:], *self.b)
            part[a, low] = added(part[a, low], ra[4], rb[0]).astype(BF16)
            part[b, high] = added(part[b, high], ra[5], rb[1]).astype(BF16)
            go(*self.c)

        def close(self):
            arrived(*self.c, self.last)
            return added(
                self.part[self.zz + self.r], self.rc[0], self.rc[1], self.zbuf[...]
            )

    ps = Balanced(ppart, pa, pb, pc, psum, pz, loop_dev, zh, y)
    ds = Scatter(dpart, dr1, dr2, dsum, dz, tp_dev, zl, x)

    arrived(*g.forward[1])
    input_term((1 - zh) * RING + across(y))
    go(*ds.first[0], *ds.first[1])
    arrived(*xg.forward[1])
    project((1 - zl) * RING + across(x))
    go(*ps.a)

    def transpose_tokens(s, carry):
        b = block_of(s)
        tokens_t = xbuf[s].astype(F32).T
        row = kinds[b].astype(F32)[0:1]
        span = pl.ds(pl.multiple_of(b * rows, rows), rows)
        for m in range(KINDS):
            xt[pl.ds(m * feat, feat), span] = jnp.where(row == m, tokens_t, 0.0).astype(BF16)
        return carry
    lax.fori_loop(0, BLOCKS, transpose_tokens, 0)

    gall = gbuf.reshape(BLOCKS * rows, cols)
    wcopies = [copy(wsend.at[m], wrecv.at[m], mate) for m in range(KINDS)]

    def wtile(m, which):
        span = pl.ds(pl.multiple_of(m * chip_rows + which * wrows, wrows), wrows)
        return jnp.dot(xt[span, :], gall[...], preferred_element_type=F32)

    def wside(m, carry):
        wsend[m] = wtile(m, 1 - core).astype(BF16)
        return carry

    def wkeep(m, carry):
        wown[m] = wtile(m, core)
        return carry

    ds.relay(0)
    ps.relay()
    lax.fori_loop(0, 2, wside, 0)
    ds.relay(1)
    lax.fori_loop(2, KINDS, wside, 0)
    go(*wcopies)
    dsum[...] = ds.close(0).astype(BF16)
    go(ds.last)
    ps.middle()
    lax.fori_loop(0, 2, wkeep, 0)
    ps.near()
    lax.fori_loop(2, KINDS, wkeep, 0)

    final = ds.close(1)
    arrived(ds.last)
    dfin[...] = (final + dz[...].astype(F32)).astype(BF16)
    turns = [
        Move(dfin.at[part], dmid.at[part], turn, turn_moves, 5 + i)
        for i, part in enumerate((low, high))
    ]
    slides = [
        Move(dmid.at[part], din_ref.at[part], slide_to, slide_moves, 7 + i)
        for i, part in enumerate((low, high))
    ]
    for t in turns:
        t.start()

    scale = float(2 * BLOCKS * rows) ** -0.5
    for m in range(KINDS):
        arrived(wcopies[m])
        wg_ref[m] = ((wown[m] + wrecv[m].astype(F32)) * scale).astype(BF16)

    for t, s in zip(turns, slides):
        t.arrived()
        s.start()

    proj_ref[...] = ps.close().astype(BF16)
    for s in slides:
        s.arrived()
    for move in flips + turns + slides:
        move.sent()
    for c in started:
        c.wait_send()


def settle(a, b, c, a_out, b_out, c_out, a_mid, b_mid, c_mid, in_sem, out_sem):
    moves = [(c.at[m], c_mid.at[m], c_out.at[m]) for m in range(c.shape[0])]
    moves += [(a, a_mid, a_out), (b, b_mid, b_out)]
    loads = [pltpu.make_async_copy(src, mid, in_sem.at[i]) for i, (src, mid, _) in enumerate(moves)]
    stores = [pltpu.make_async_copy(mid, dst, out_sem.at[i]) for i, (_, mid, dst) in enumerate(moves)]
    for load in loads:
        load.start()
    for load, store in zip(loads, stores):
        load.wait()
        store.start()
    for store in stores:
        store.wait()


def per_device(tokens, out_grad, qkv_weight, dest_row, loop_modality):
    rows, feat = tokens.shape
    cols = out_grad.shape[1]
    kinds, wrows, _ = qkv_weight.shape
    half = rows // 2
    any_spec = pl.BlockSpec(memory_space=pl.ANY)
    vmem = pl.BlockSpec(memory_space=pltpu.VMEM)
    deep = kinds * 2 * wrows

    shapes = (
        jax.ShapeDtypeStruct((rows, cols), BF16),
        jax.ShapeDtypeStruct((rows, feat), BF16),
        jax.ShapeDtypeStruct(qkv_weight.shape, BF16),
    )
    results = pl.pallas_call(
        kernel,
        out_shape=shapes,
        in_specs=[any_spec, any_spec, any_spec, vmem, pl.BlockSpec(memory_space=pltpu.SMEM)],
        out_specs=(vmem, vmem, vmem),
        scratch_shapes=[
            pltpu.VMEM((BLOCKS, META, rows), BF16),
            pltpu.VMEM((BLOCKS, rows, feat), BF16),
            pltpu.VMEM((BLOCKS, rows, cols), BF16),
            pltpu.VMEM((deep, cols), BF16),
            pltpu.VMEM((cols, deep), BF16),
            pltpu.VMEM((deep, BLOCKS * rows), BF16),
            pltpu.VMEM((BLOCKS, rows, cols), BF16),
            pltpu.VMEM((6, half, cols), BF16),
            pltpu.VMEM((2, half, cols), BF16),
            pltpu.VMEM((2, rows, cols), BF16),
            pltpu.VMEM((rows, cols), BF16),
            pltpu.VMEM((rows, cols), BF16),
            pltpu.VMEM((BLOCKS, rows, feat), BF16),
            pltpu.VMEM((2, 2, half, feat), BF16),
            pltpu.VMEM((2, 2, rows, feat), BF16),
            pltpu.VMEM((rows, feat), BF16),
            pltpu.VMEM((rows, feat), BF16),
            pltpu.VMEM((rows, feat), BF16),
            pltpu.VMEM((rows, feat), BF16),
            pltpu.VMEM((kinds, wrows, cols), F32),
            pltpu.VMEM((kinds, wrows, cols), BF16),
            pltpu.VMEM((kinds, wrows, cols), BF16),
            pltpu.SemaphoreType.DMA((9,)),
            pltpu.SemaphoreType.DMA((80,)),
            pltpu.SemaphoreType.DMA((80,)),
        ],
        compiler_params=pltpu.CompilerParams(
            collective_id=0, has_side_effects=True, vmem_limit_bytes=60 * 1024 * 1024
        ),
        name="stationary",
    )(tokens, out_grad, qkv_weight, dest_row.reshape(1, rows), loop_modality)
    return pl.pallas_call(
        settle,
        out_shape=shapes,
        in_specs=[any_spec] * 3,
        out_specs=(any_spec,) * 3,
        scratch_shapes=[
            *(pltpu.VMEM(shape.shape, BF16) for shape in shapes),
            pltpu.SemaphoreType.DMA((kinds + 2,)),
            pltpu.SemaphoreType.DMA((kinds + 2,)),
        ],
        name="settle",
    )(*results)


def solution(mesh):
    placed = (P("loop", "tp"), P("loop", "tp"), P(None, "loop", "tp"), P("loop"), P())
    return jax.shard_map(
        per_device,
        mesh=mesh,
        in_specs=placed,
        out_specs=(P("loop", "tp"), P("loop", "tp"), P(None, "loop", "tp")),
        check_vma=False,
    )
```

```python
import jax
import jax.numpy as jnp
from jax import lax
from jax.experimental import pallas as pl
from jax.experimental.pallas import tpu as pltpu
from jax.sharding import PartitionSpec as P

MESH = pl.DeviceIdType.MESH
F32, BF16 = jnp.float32, jnp.bfloat16
RING = 4
BLOCKS = 8
KINDS = 3
GROUPS = 2
META = 16


def kernel(
    tok_ref, grad_ref, w_ref, dest_ref, kind_ref,
    proj_ref, din_ref, wg_ref,
    kinds, xbuf, gbuf, wbuf, wtbuf, xt,
    ppart, pa, pb, pc, psum, pz,
    dpart, dr1, dr2, dsum, dz, dfin, dmid,
    wown, wsend, wrecv,
    local_sem, send_sem, recv_sem,
):
    rows, feat = tok_ref.shape
    cols = grad_ref.shape[1]
    wrows = w_ref.shape[1]
    chip_rows = 2 * wrows
    size = rows // GROUPS
    half = size // 2
    low, high = pl.ds(0, half), pl.ds(half, half)
    part_rows = [pl.ds(h * size, size) for h in range(GROUPS)]

    loop_id = lax.axis_index("loop")
    tp_id = lax.axis_index("tp")
    core = lax.rem(loop_id, 2)
    chip = lax.div(loop_id, 2)
    zh, y = lax.div(chip, RING), lax.rem(chip, RING)
    zl, x = lax.div(tp_id, RING), lax.rem(tp_id, RING)

    def at(a, b):
        return {"loop": a * 2 + core, "tp": b}

    def loop_dev(z, r):
        return at(z * RING + r, tp_id)

    def tp_dev(z, r):
        return at(chip, z * RING + r)

    mate = {"loop": chip * 2 + (1 - core), "tp": tp_id}
    plus, minus = lax.rem(x + y, RING), lax.rem(x - y + RING, RING)
    flip_to = at(zl * RING + x, zh * RING + plus)
    flip_from = at(zl * RING + minus, zh * RING + y)
    flip_moves = jnp.logical_not((zh == zl) & (x == y) & (y == 0))
    turn = at(zl * RING + minus, zh * RING + x)
    turn_moves = jnp.logical_not((zh == zl) & (minus == y))
    slide_to = at(chip, zl * RING + minus)
    slide_from = at(chip, zl * RING + plus)
    slide_moves = y != 0

    def slot_of(b):
        return lax.div(b, RING) * RING + lax.rem(lax.rem(b, RING) + y, RING)

    def block_of(s):
        return lax.div(s, RING) * RING + lax.rem(lax.rem(s, RING) - y + RING, RING)

    def right(r):
        return lax.rem(r + 1, RING)

    def left(r):
        return lax.rem(r + RING - 1, RING)

    def across(r):
        return lax.rem(r + 2, RING)

    count = [0]
    started = []

    def copy(src, dst, device):
        i = count[0]
        count[0] += 1
        return pltpu.make_async_remote_copy(
            src_ref=src, dst_ref=dst, send_sem=send_sem.at[i], recv_sem=recv_sem.at[i],
            device_id=device, device_id_type=MESH,
        )

    def go(*copies):
        for c in copies:
            c.start()
            started.append(c)

    def arrived(*copies):
        for c in copies:
            c.wait_recv()

    class Move:
        def __init__(self, src, dst, device, moves, sem):
            self.remote = copy(src, dst, device)
            self.local = pltpu.make_async_copy(src, dst, local_sem.at[sem])
            self.moves = moves

        def start(self):
            pl.when(self.moves)(self.remote.start)
            pl.when(jnp.logical_not(self.moves))(self.local.start)

        def arrived(self):
            pl.when(self.moves)(self.remote.wait_recv)
            pl.when(jnp.logical_not(self.moves))(self.local.wait)

        def sent(self):
            pl.when(self.moves)(self.remote.wait_send)

    barrier = pltpu.get_barrier_semaphore()

    def greet(device):
        pl.semaphore_signal(barrier, inc=1, device_id=device, device_id_type=MESH)

    loop_peers = []
    for i in range(1, BLOCKS):
        z = lax.rem(zh + i // RING, 2)
        loop_peers.append(loop_dev(z, lax.rem(y + i % RING, RING)))
    for peer in loop_peers + [mate, tp_dev(1 - zl, x), tp_dev(zl, right(x)), tp_dev(zl, left(x))]:
        greet(peer)

    @pl.when(flip_moves)
    def _():
        greet(flip_to)
        greet(flip_from)

    @pl.when(turn_moves)
    def _():
        greet(turn)

    @pl.when(slide_moves)
    def _():
        greet(slide_to)
        greet(slide_from)

    load_g = [
        pltpu.make_async_copy(grad_ref.at[part_rows[h]], gbuf.at[h, chip], local_sem.at[h])
        for h in range(GROUPS)
    ]
    for c in load_g:
        c.start()
    load_w = []
    for m in range(KINDS):
        own_rows = pl.ds(m * chip_rows + core * wrows, wrows)
        load_w.append(pltpu.make_async_copy(w_ref.at[m], wbuf.at[own_rows], local_sem.at[2 + m]))
        load_w[-1].start()

    dest = dest_ref[...]
    kind = jnp.full(dest.shape, kind_ref[0], jnp.int32)
    for i in range(1, 2 * BLOCKS):
        kind = jnp.where(dest >= i * (3 * rows // (4 * BLOCKS)), kind_ref[i], kind)
    top = lax.broadcasted_iota(jnp.int32, (META, rows), 0) == 0
    kinds[chip] = jnp.where(top, kind.astype(F32), 0.0).astype(BF16)

    expected = len(loop_peers) + 4 + jnp.where(flip_moves, 2, 0)
    pl.semaphore_wait(
        barrier, expected + jnp.where(turn_moves, 1, 0) + jnp.where(slide_moves, 2, 0)
    )

    flips = [
        Move(tok_ref.at[part_rows[h]], xbuf.at[h, zh * RING + plus], flip_to, flip_moves, 5 + h)
        for h in range(GROUPS)
    ]

    class Gather:
        def __init__(self, buf, dev, z, r, src, balanced):
            own, other = z * RING + r, (1 - z) * RING + r
            first = buf.at[own] if src is None else src
            to_right, to_left, over = dev(z, right(r)), dev(z, left(r)), dev(1 - z, r)
            self.z = copy(first, buf.at[own], over)
            self.own = [copy(first, buf.at[own], to) for to in (to_right, to_left)]
            self.forward, self.cross = [], []
            for zz in (z, 1 - z):
                a, b = buf.at[zz * RING + left(r), low], buf.at[zz * RING + right(r), high]
                self.forward.append([copy(a, a, to_right), copy(b, b, to_left)])
                if balanced and not self.cross:
                    self.cross = [copy(a, a, over), copy(b, b, over)]
            a, b = (buf.at[other, high], buf.at[other, low]) if balanced else (buf.at[other],) * 2
            self.other = [copy(a, a, to_right), copy(b, b, to_left)]

        def begin(self):
            go(self.z, *self.own)

        def ring(self):
            arrived(*self.own)
            go(*self.forward[0], *self.cross)

        def plane(self):
            arrived(self.z)
            go(*self.other)

        def crossed(self):
            arrived(*(self.cross or self.other))
            go(*self.forward[1])

        def ends(self):
            arrived(*self.forward[0], *self.forward[1])

    g = [Gather(gbuf.at[h], loop_dev, zh, y, grad_ref.at[part_rows[h]], True) for h in range(GROUPS)]
    xg = [Gather(xbuf.at[h], tp_dev, zl, x, None, False) for h in range(GROUPS)]
    tell = [copy(kinds.at[chip], kinds.at[chip], peer) for peer in loop_peers]
    wswap = []
    for m in range(KINDS):
        own_rows = pl.ds(m * chip_rows + core * wrows, wrows)
        wswap.append(copy(w_ref.at[m], wbuf.at[own_rows], mate))

    ones = jnp.ones((META, 128), BF16)

    def kind_columns(b, h, width):
        col = lax.dot_general(
            kinds[b, :, part_rows[h]], ones, (((0,), (0,)), ((), ())), preferred_element_type=F32
        )
        return jnp.concatenate([col] * (width // 128), axis=1)

    def project(h, s, t):
        b, c = block_of(s), block_of(t)
        tokens = jnp.concatenate([xbuf[h, s], xbuf[h, t]], axis=0).astype(F32)
        col = jnp.concatenate([kind_columns(b, h, feat), kind_columns(c, h, feat)], axis=0)
        stacked = jnp.concatenate(
            [jnp.where(col == m, tokens, 0.0).astype(BF16) for m in range(KINDS)], axis=1
        )
        out = jnp.dot(stacked, wbuf[...], preferred_element_type=F32).astype(BF16)
        ppart[h, b] = out[:size]
        ppart[h, c] = out[size:]

    def input_term(h, b, c):
        grads = jnp.concatenate([gbuf[h, b], gbuf[h, c]], axis=0)
        out = jnp.dot(grads, wtbuf[...], preferred_element_type=F32)
        col = jnp.concatenate([kind_columns(b, h, feat), kind_columns(c, h, feat)], axis=0)
        picked = jnp.where(
            col == 0, out[:, :feat], jnp.where(col == 1, out[:, feat:2 * feat], out[:, 2 * feat:])
        ).astype(BF16)
        dpart[h, slot_of(b)] = picked[:size]
        dpart[h, slot_of(c)] = picked[size:]

    def pairs(z, r):
        o = 1 - z
        return dict(
            near=(z * RING + right(r), z * RING + left(r)),
            home=(z * RING + r, o * RING + r),
            side=(o * RING + right(r), o * RING + left(r)),
            far=(z * RING + across(r), o * RING + across(r)),
        )

    gp, xp = pairs(zh, y), pairs(zl, x)

    def added(a, *others):
        total = a.astype(F32)
        for o in others:
            total = total + o.astype(F32)
        return total

    class Scatter:
        def __init__(self, part, r1, r2, total, zbuf, dev, z, r):
            self.part, self.r1, self.r2, self.total, self.zbuf = part, r1, r2, total, zbuf
            self.z, self.r = z, r
            self.first, self.second = [], []
            for i, zz in enumerate((1 - z, z)):
                far = zz * RING + across(r)
                self.first.append([
                    copy(part.at[far, low], r1.at[i, 0], dev(z, right(r))),
                    copy(part.at[far, high], r1.at[i, 1], dev(z, left(r))),
                ])
                self.second.append([
                    copy(part.at[zz * RING + right(r)], r2.at[i, 0], dev(z, right(r))),
                    copy(part.at[zz * RING + left(r)], r2.at[i, 1], dev(z, left(r))),
                ])
            self.last = copy(total, zbuf, dev(1 - z, r))

        def block(self, i, step):
            zz = (1 - self.z) if i == 0 else self.z
            return zz * RING + lax.rem(self.r + step, RING)

        def begin(self):
            go(*self.first[0], *self.first[1])

        def relay(self, i):
            arrived(*self.first[i])
            a, b = self.block(i, 1), self.block(i, 3)
            self.part[a, low] = added(self.part[a, low], self.r1[i, 0]).astype(BF16)
            self.part[b, high] = added(self.part[b, high], self.r1[i, 1]).astype(BF16)
            go(*self.second[i])

        def close(self, i):
            arrived(*self.second[i])
            return added(self.part[self.block(i, 0)], self.r2[i, 0], self.r2[i, 1])

    class Balanced:
        def __init__(self, part, ra, rb, rc, total, zbuf, dev, z, r):
            o = 1 - z
            self.part, self.ra, self.rb, self.rc, self.total, self.zbuf = part, ra, rb, rc, total, zbuf
            self.l, self.r_, self.r = left(r), right(r), r
            far = across(r)
            to_left, to_right, over = dev(z, left(r)), dev(z, right(r)), dev(o, r)
            oo, zz = o * RING, z * RING
            self.a = [
                copy(part.at[oo + far, low], ra.at[0], to_left),
                copy(part.at[oo + far, high], ra.at[1], to_right),
                copy(part.at[oo + self.l, high], ra.at[2], to_left),
                copy(part.at[oo + self.r_, low], ra.at[3], to_right),
                copy(part.at[zz + far, low], ra.at[4], to_left),
                copy(part.at[zz + far, high], ra.at[5], to_right),
            ]
            self.b = [
                copy(part.at[oo + self.l, low], rb.at[0], over),
                copy(part.at[oo + self.r_, high], rb.at[1], over),
            ]
            self.last = copy(total, zbuf, over)
            self.c = [
                copy(part.at[zz + self.l], rc.at[0], to_left),
                copy(part.at[zz + self.r_], rc.at[1], to_right),
            ]
            self.oo, self.zz = oo, zz

        def begin(self):
            go(*self.a)

        def relay(self):
            part, ra = self.part, self.ra
            a, b = self.oo + self.l, self.oo + self.r_
            arrived(*self.a[:2])
            part[a, low] = added(part[a, low], ra[0]).astype(BF16)
            part[b, high] = added(part[b, high], ra[1]).astype(BF16)
            go(*self.b)

        def middle(self):
            part, ra = self.part, self.ra
            own = self.oo + self.r
            arrived(*self.a[2:4])
            self.total[low] = added(part[own, low], ra[3]).astype(BF16)
            self.total[high] = added(part[own, high], ra[2]).astype(BF16)
            go(self.last)

        def near(self):
            part, ra, rb = self.part, self.ra, self.rb
            a, b = self.zz + self.l, self.zz + self.r_
            arrived(*self.a[4:], *self.b)
            part[a, low] = added(part[a, low], ra[4], rb[0]).astype(BF16)
            part[b, high] = added(part[b, high], ra[5], rb[1]).astype(BF16)
            go(*self.c)

        def close(self):
            arrived(*self.c, self.last)
            return added(
                self.part[self.zz + self.r], self.rc[0], self.rc[1], self.zbuf[...]
            )

    ps = [
        Balanced(
            ppart.at[h], pa.at[h], pb.at[h], pc.at[h], psum.at[h], pz.at[h], loop_dev, zh, y
        )
        for h in range(GROUPS)
    ]
    ds = [
        Scatter(dpart.at[h], dr1.at[h], dr2.at[h], dsum.at[h], dz.at[h], tp_dev, zl, x)
        for h in range(GROUPS)
    ]
    turns = [Move(dfin.at[h], dmid.at[h], turn, turn_moves, 7 + h) for h in range(GROUPS)]
    slides = [
        Move(dmid.at[h], din_ref.at[part_rows[h]], slide_to, slide_moves, 9 + h)
        for h in range(GROUPS)
    ]

    def d_plane(h):
        dsum[h] = ds[h].close(0).astype(BF16)
        go(ds[h].last)

    def d_turn(h):
        final = ds[h].close(1)
        arrived(ds[h].last)
        dfin[h] = (final + dz[h].astype(F32)).astype(BF16)
        turns[h].start()

    def d_slide(h):
        turns[h].arrived()
        slides[h].start()

    def p_close(h):
        proj_ref[part_rows[h]] = ps[h].close().astype(BF16)

    def transpose_tokens(h):
        def body(s, carry):
            b = block_of(s)
            tokens_t = xbuf[h, s].astype(F32).T
            row = kinds[b, :, part_rows[h]].astype(F32)[0:1]
            span = pl.ds(pl.multiple_of((h * BLOCKS + b) * size, size), size)
            for m in range(KINDS):
                xt[pl.ds(m * feat, feat), span] = jnp.where(row == m, tokens_t, 0.0).astype(BF16)
            return carry
        lax.fori_loop(0, BLOCKS, body, 0)

    gall = gbuf.reshape(GROUPS * BLOCKS * size, cols)
    wcopies = [copy(wsend.at[m], wrecv.at[m], mate) for m in range(KINDS)]

    def wtile(m, which):
        span = pl.ds(pl.multiple_of(m * chip_rows + which * wrows, wrows), wrows)
        return jnp.dot(xt[span, :], gall[...], preferred_element_type=F32)

    def wside(m, carry):
        wsend[m] = wtile(m, 1 - core).astype(BF16)
        return carry

    def wkeep(m, carry):
        wown[m] = wtile(m, core)
        return carry

    def turn_weights(m, carry):
        span = pl.ds(pl.multiple_of(m * chip_rows, chip_rows), chip_rows)
        wtbuf[:, span] = wbuf[span, :].T
        return carry

    flips[0].start()
    go(*tell)
    g[0].begin()
    go(*wswap)
    for c in load_w + load_g:
        c.wait()
    arrived(*wswap)
    lax.fori_loop(0, KINDS, turn_weights, 0)

    flips[0].arrived()
    xg[0].begin()
    flips[1].start()
    g[1].begin()
    g[0].ring()
    g[0].plane()
    xg[0].ring()
    xg[0].plane()
    arrived(*tell)
    input_term(0, *gp["near"])
    project(0, *xp["near"])
    flips[1].arrived()
    xg[1].begin()
    input_term(0, *gp["home"])
    project(0, *xp["home"])
    g[0].crossed()
    xg[0].crossed()
    g[1].ring()
    arrived(*g[0].other)
    input_term(0, *gp["side"])
    g[1].plane()
    project(0, *xp["side"])
    xg[1].ring()
    xg[1].plane()
    g[0].ends()
    input_term(0, *gp["far"])
    ds[0].begin()
    xg[0].ends()
    project(0, *xp["far"])
    ps[0].begin()
    input_term(1, *gp["near"])
    project(1, *xp["near"])
    g[1].crossed()
    xg[1].crossed()
    ds[0].relay(0)
    ps[0].relay()
    input_term(1, *gp["home"])
    ds[0].relay(1)
    project(1, *xp["home"])
    arrived(*g[1].other)
    input_term(1, *gp["side"])
    d_plane(0)
    ps[0].middle()
    project(1, *xp["side"])
    ps[0].near()
    g[1].ends()
    input_term(1, *gp["far"])
    ds[1].begin()
    xg[1].ends()
    project(1, *xp["far"])
    ps[1].begin()
    transpose_tokens(0)
    ds[1].relay(0)
    ps[1].relay()
    d_turn(0)
    transpose_tokens(1)
    ds[1].relay(1)
    lax.fori_loop(0, 2, wside, 0)
    d_plane(1)
    ps[1].middle()
    lax.fori_loop(2, KINDS, wside, 0)
    go(*wcopies)
    ps[1].near()
    d_slide(0)
    p_close(0)
    lax.fori_loop(0, 1, wkeep, 0)
    d_turn(1)
    lax.fori_loop(1, KINDS, wkeep, 0)
    d_slide(1)

    scale = float(2 * BLOCKS * rows) ** -0.5
    for m in range(KINDS):
        arrived(wcopies[m])
        wg_ref[m] = ((wown[m] + wrecv[m].astype(F32)) * scale).astype(BF16)

    p_close(1)
    for s in slides:
        s.arrived()
    for move in flips + turns + slides:
        move.sent()
    for c in started:
        c.wait_send()


def settle(a, b, c, a_out, b_out, c_out, a_mid, b_mid, c_mid, in_sem, out_sem):
    moves = [(c.at[m], c_mid.at[m], c_out.at[m]) for m in range(c.shape[0])]
    moves += [(a, a_mid, a_out), (b, b_mid, b_out)]
    loads = [pltpu.make_async_copy(src, mid, in_sem.at[i]) for i, (src, mid, _) in enumerate(moves)]
    stores = [pltpu.make_async_copy(mid, dst, out_sem.at[i]) for i, (_, mid, dst) in enumerate(moves)]
    for load in loads:
        load.start()
    for load, store in zip(loads, stores):
        load.wait()
        store.start()
    for store in stores:
        store.wait()


def per_device(tokens, out_grad, qkv_weight, dest_row, loop_modality):
    rows, feat = tokens.shape
    cols = out_grad.shape[1]
    kinds, wrows, _ = qkv_weight.shape
    size = rows // GROUPS
    half = size // 2
    any_spec = pl.BlockSpec(memory_space=pl.ANY)
    vmem = pl.BlockSpec(memory_space=pltpu.VMEM)
    deep = kinds * 2 * wrows

    shapes = (
        jax.ShapeDtypeStruct((rows, cols), BF16),
        jax.ShapeDtypeStruct((rows, feat), BF16),
        jax.ShapeDtypeStruct(qkv_weight.shape, BF16),
    )
    results = pl.pallas_call(
        kernel,
        out_shape=shapes,
        in_specs=[any_spec, any_spec, any_spec, vmem, pl.BlockSpec(memory_space=pltpu.SMEM)],
        out_specs=(vmem, vmem, vmem),
        scratch_shapes=[
            pltpu.VMEM((BLOCKS, META, rows), BF16),
            pltpu.VMEM((GROUPS, BLOCKS, size, feat), BF16),
            pltpu.VMEM((GROUPS, BLOCKS, size, cols), BF16),
            pltpu.VMEM((deep, cols), BF16),
            pltpu.VMEM((cols, deep), BF16),
            pltpu.VMEM((deep, BLOCKS * rows), BF16),
            pltpu.VMEM((GROUPS, BLOCKS, size, cols), BF16),
            pltpu.VMEM((GROUPS, 6, half, cols), BF16),
            pltpu.VMEM((GROUPS, 2, half, cols), BF16),
            pltpu.VMEM((GROUPS, 2, size, cols), BF16),
            pltpu.VMEM((GROUPS, size, cols), BF16),
            pltpu.VMEM((GROUPS, size, cols), BF16),
            pltpu.VMEM((GROUPS, BLOCKS, size, feat), BF16),
            pltpu.VMEM((GROUPS, 2, 2, half, feat), BF16),
            pltpu.VMEM((GROUPS, 2, 2, size, feat), BF16),
            pltpu.VMEM((GROUPS, size, feat), BF16),
            pltpu.VMEM((GROUPS, size, feat), BF16),
            pltpu.VMEM((GROUPS, size, feat), BF16),
            pltpu.VMEM((GROUPS, size, feat), BF16),
            pltpu.VMEM((kinds, wrows, cols), F32),
            pltpu.VMEM((kinds, wrows, cols), BF16),
            pltpu.VMEM((kinds, wrows, cols), BF16),
            pltpu.SemaphoreType.DMA((11,)),
            pltpu.SemaphoreType.DMA((112,)),
            pltpu.SemaphoreType.DMA((112,)),
        ],
        compiler_params=pltpu.CompilerParams(
            collective_id=0, has_side_effects=True, vmem_limit_bytes=60 * 1024 * 1024
        ),
        name="stationary",
    )(tokens, out_grad, qkv_weight, dest_row.reshape(1, rows), loop_modality)
    return pl.pallas_call(
        settle,
        out_shape=shapes,
        in_specs=[any_spec] * 3,
        out_specs=(any_spec,) * 3,
        scratch_shapes=[
            *(pltpu.VMEM(shape.shape, BF16) for shape in shapes),
            pltpu.SemaphoreType.DMA((kinds + 2,)),
            pltpu.SemaphoreType.DMA((kinds + 2,)),
        ],
        name="settle",
    )(*results)


def solution(mesh):
    placed = (P("loop", "tp"), P("loop", "tp"), P(None, "loop", "tp"), P("loop"), P())
    return jax.shard_map(
        per_device,
        mesh=mesh,
        in_specs=placed,
        out_specs=(P("loop", "tp"), P("loop", "tp"), P(None, "loop", "tp")),
        check_vma=False,
    )
```
